32 devices in a mesh: groups: 2 (over y), tm: 4 (over z), space: 2 (over x), clip: 2 (over core).
Axes of the slice: x: 2, y: 2, z: 4, core: 2. Of those that a mesh axis runs over, the one named last changes fastest.
Arguments:
- features: bfloat16 [4, 16, 8, 16, 256], P(('groups', 'clip'), 'tm', 'space'), parts along dimension 0, may hold values from -6 to 6
- frame_counts: int32 [4], P(('groups', 'clip')), parts along dimension 0, may hold values from 1 to 16, as said below
- routes: int32 [4, 512, 1], P(('groups', 'clip'), ('tm', 'space')), parts along dimension 0, may hold values from 0 to 7; in each aligned block of 64 rows (0 to 63, 64 to 127, ..., all dimensions but the last counted through in order) at most 9 rows name the same one
- norm_gains: float32 [3, 256], replicated, may hold values from 0.5 to 1.5
- conv_weights: bfloat16 [2, 256, 27, 256], P(None, 'tm'), may hold values from -0.078125 to 0.078125
- conv_biases: float32 [2, 256], replicated, may hold values from -3 to 3
- latent_weight: bfloat16 [256, 16], replicated, may hold values from -0.375 to 0.375
- embed_weight: bfloat16 [64, 3072], replicated, may hold values from -0.75 to 0.75
- embed_bias: float32 [3072], replicated, may hold values from -3 to 3
Outputs:
- packed: bfloat16 [4, 576, 3072], P(('groups', 'clip'), ('tm', 'space')), parts along dimension 0
The draws below stay inside these ranges and needn't reach their ends.
There are 2 independent parts, one for each index of `groups`. The reference program is written for one: setup_inputs(seed, part) draws one part's arguments, and reference() takes and returns one part's arrays. A program takes and returns all parts, laid end to end along the dimension named above; an argument that names none is the same for every part. Nothing has to cross between parts.
Inputs may be any that keep to these rules, and one draw needn't show every extreme that they name: `routes`: in each clip, the 64 patches of one span and tile name any one owner at most 9 times. `frame_counts`: one clip of each part has all 16 frames valid.
All inputs are finite; a program needn't handle non-finite values.
Results may differ from the reference program's by a relative error of at most 0.0054.
Values may be sent and summed in bfloat16 or wider, within the bound.
A program may use at most 64 MiB of HBM per device.

```python
import math
import jax
import jax.numpy as jnp
import numpy as np
from jax import lax

C = 256
LAT = 16
EMBED = 3072
FR = 4
ROWS = 4
COLS = 16
CLIPS = 2
FRAMES = 16
ROWS_ALL = 8
OWNERS = 8
TOK_DEV = 64
PATCHES = 512
MOST = 9
SLOTS = 72
N_TM = 4
N_SPACE = 2


def draw_frame_counts(key, part):
    first_key, second_key = jax.random.split(jax.random.fold_in(key, 17))
    counts = jax.random.randint(first_key, (CLIPS,), 1, FRAMES + 1)
    chosen = jax.random.randint(second_key, (), 0, CLIPS)
    return jnp.where(jnp.arange(CLIPS) == chosen, FRAMES, counts).astype(jnp.int32)


def levels(key, dims, shards, least, top_value):
    def one(position, parts):
        heights = jax.random.uniform(jax.random.fold_in(jax.random.fold_in(key, 6), position), (parts,), jnp.float32, least / len(shards), top_value / len(shards))
        return jnp.repeat(jnp.exp(heights), dims[position] // parts).reshape((-1,) + (1,) * (len(dims) - position - 1))

    level = one(*shards[0])
    for cut in shards[1:]:
        level = level * one(*cut)
    return level


def routed_block(key, own, number, rows, count, top, bound, skew):
    sequence = jax.random.permutation(key, count)
    heavy_load, usual = portions_of(count, rows * top, bound, skew, True), portions_of(count, rows * top, bound, skew, False)
    places = jnp.arange(count)

    def named(tallies, rotation):
        used = int((tallies > 0).sum())
        fixed = max(1, used // 4)
        moved = fixed + (places - fixed + rotation * (used - fixed)) % max(1, count - fixed)
        return jnp.zeros((count,), jnp.int32).at[sequence[jnp.where(places < fixed, places, moved)]].set(jnp.asarray(tallies, jnp.int32))

    tallies = jnp.where(number % 4 == 0, named(heavy_load, number // 4), named(usual, number - number // 4 - 1))
    mixed = jax.random.permutation(jax.random.fold_in(own, 3), count)
    giver, receiver = mixed[0:count // 2 * 2:2], mixed[1:count // 2 * 2:2]
    slack = jnp.minimum(tallies[giver] - 1, bound - tallies[receiver]) // 2
    slack = jnp.where((giver == sequence[0]) | (receiver == sequence[0]) | (tallies[receiver] == 0), 0, jnp.maximum(slack, 0))
    moved = jax.random.randint(jax.random.fold_in(own, 4), (count // 2,), 0, 1 << 20) % (slack + 1)
    tallies = tallies.at[giver].add(-moved).at[receiver].add(moved)
    items = jnp.searchsorted(jnp.cumsum(tallies), jnp.arange(rows * top), side="right").astype(jnp.int32)
    table = items.reshape(top, rows).T
    table = table[jax.random.permutation(jax.random.fold_in(own, 1), rows)]
    rotation = jax.random.randint(jax.random.fold_in(own, 2), (rows, 1), 0, top)
    return jnp.take_along_axis(table, (jnp.arange(top)[None, :] + rotation) % top, axis=1)


def portions_of(number_of, total, limit, slope, full):
    weights = [(1 << 20) // math.isqrt(rank ** slope) + 1 for rank in range(1, number_of + 1)]
    largest = limit if full else min(limit, max(-(-total // number_of), total * weights[0] // sum(weights)))
    least = 1 if total - largest >= number_of - 1 else 0
    given, surplus = [largest] + [least] * (number_of - 1), total - largest - least * (number_of - 1)
    while surplus > 0:
        candidates = [i for i in range(1, number_of) if given[i] < largest] or [i for i in range(1, number_of) if given[i] < limit]
        whole, budget = sum([weights[i] for i in candidates]), surplus
        for i in candidates:
            extra = min(limit - given[i], max(1, budget * weights[i] // whole), surplus)
            given[i] = given[i] + extra
            surplus = surplus - extra
    return np.array(given)


def noise(rng, extent, deviation, bound, shards=(), held_as=jnp.bfloat16):
    entries = deviation * jax.random.normal(rng, extent, jnp.float32)
    if shards:
        entries = entries * levels(rng, extent, shards, -0.22, 0.18)
    return jnp.clip(entries, -bound, bound).astype(held_as)


def setup_inputs(seed: int = 0, part: int = 0) -> dict:
    key_of = jax.random.split(jax.random.key(seed), 10)
    part_splits = jax.random.split(jax.random.fold_in(key_of[9], part), 10)
    features = noise(part_splits[0], (CLIPS, FRAMES, ROWS_ALL, COLS, C), 1.0, 6.0, ((0, 2), (1, 4), (2, 2)))
    frame_counts = draw_frame_counts(jax.random.fold_in(jax.random.fold_in(key_of[9], part), 71), part)
    routes_keys = jax.random.split(jax.random.fold_in(part_splits[2], 1), CLIPS * PATCHES // TOK_DEV)
    routes_turns = jax.random.permutation(jax.random.fold_in(part_splits[2], 3), CLIPS * PATCHES // TOK_DEV)
    routes = jax.vmap(lambda own, number: routed_block(jax.random.fold_in(part_splits[2], 2), own, number, TOK_DEV, OWNERS, 1, MOST, 2))(routes_keys, routes_turns).reshape((CLIPS, PATCHES, 1))
    norm_gains = jnp.clip(jax.random.uniform(key_of[3], (3, C), jnp.float32, 0.5, 1.5), 0.5, 1.5)
    conv_weights = noise(key_of[4], (2, C, 27, C), (27 * C) ** -0.5, 0.078125, ((1, 4),))
    conv_biases = noise(key_of[5], (2, C), 0.5, 3.0, (), jnp.float32)
    latent_weight = noise(key_of[6], (C, LAT), C ** -0.5, 0.375)
    embed_weight = noise(key_of[7], (4 * LAT, EMBED), (4 * LAT) ** -0.5, 0.75)
    embed_bias = noise(key_of[8], (EMBED,), 0.5, 3.0, (), jnp.float32)
    return dict(features=features, frame_counts=frame_counts, routes=routes, norm_gains=norm_gains, conv_weights=conv_weights, conv_biases=conv_biases, latent_weight=latent_weight, embed_weight=embed_weight, embed_bias=embed_bias)


def norm_silu(values, gain):
    scale = lax.rsqrt(lax.optimization_barrier(jnp.mean(values * values, axis=-1, keepdims=True)) + 1e-06)
    return jax.nn.silu(values * scale * gain)

def causal_conv(inputs, weights):
    kernel = weights.astype(jnp.float32).reshape(C, 3, 3, 3, C).transpose(1, 2, 3, 4, 0)
    result = lax.conv_general_dilated(inputs.astype(jnp.float32)[None], kernel, (1, 1, 1), ((2, 0), (1, 1), (1, 1)), dimension_numbers=('NDHWC', 'DHWIO', 'NDHWC'), precision=lax.Precision.HIGHEST)
    return result[0]

def encode_clip(clip_features, clip_count, clip_routes, norm_gains, conv_weights, conv_biases, latent_weight, embed_weight, embed_bias):
    inputs = clip_features.astype(jnp.float32)
    active = norm_silu(inputs, norm_gains[0]).astype(jnp.bfloat16)
    hidden = causal_conv(active, conv_weights[0]) + conv_biases[0]
    active = norm_silu(hidden, norm_gains[1]).astype(jnp.bfloat16)
    hidden = causal_conv(active, conv_weights[1]) + conv_biases[1]
    merged = inputs + hidden
    active = norm_silu(merged, norm_gains[2]).astype(jnp.bfloat16)
    latent = jnp.dot(active.reshape(-1, C), latent_weight, preferred_element_type=jnp.float32)
    latent = latent.reshape(N_TM, FR, N_SPACE, ROWS // 2, 2, COLS // 2, 2, LAT)
    patches = latent.transpose(0, 2, 1, 3, 5, 4, 6, 7).reshape(PATCHES, 4 * LAT).astype(jnp.bfloat16)
    embedded = jnp.dot(patches, embed_weight, preferred_element_type=jnp.float32) + embed_bias
    destinations = clip_routes[:, 0].astype(jnp.int32)
    blocks = destinations.reshape(OWNERS, TOK_DEV)
    positions = jnp.arange(TOK_DEV).astype(jnp.int32)
    before = positions[:, None] > positions[None, :]
    matches = (blocks[:, :, None] == blocks[:, None, :]) & before[None]
    ranks = lax.optimization_barrier(jnp.sum(matches.astype(jnp.int32), axis=2)).reshape(PATCHES)
    indices = jnp.arange(PATCHES).astype(jnp.int32)
    sources = indices // TOK_DEV
    target_rows = destinations * SLOTS + sources * MOST + ranks
    frame_ids = sources // N_SPACE * FR + indices % TOK_DEV // (ROWS // 2 * (COLS // 2))
    alive = (frame_ids < clip_count).astype(jnp.float32)
    values = (embedded * alive[:, None]).astype(jnp.bfloat16)
    return jnp.zeros((OWNERS * SLOTS, EMBED), jnp.bfloat16).at[target_rows].set(values)

def reference(features, frame_counts, routes, norm_gains, conv_weights, conv_biases, latent_weight, embed_weight, embed_bias):
    results = [encode_clip(features[clip_index], frame_counts[clip_index], routes[clip_index], norm_gains, conv_weights, conv_biases, latent_weight, embed_weight, embed_bias) for clip_index in range(CLIPS)]
    return jnp.stack(results)
```

```python
import functools

import jax
import jax.numpy as jnp
from jax import lax
from jax.experimental import pallas as pl
from jax.experimental.pallas import tpu as pltpu
from jax.sharding import PartitionSpec as P

MESH = pl.DeviceIdType.MESH
LANES = 128
SUBLANES = 16


def norm_silu(values, gain):
    scale = lax.rsqrt(jnp.mean(values * values, axis=-1, keepdims=True) + 1e-06)
    scaled = values * scale * gain
    return scaled / (1.0 + jnp.exp(-scaled))


def encoder(
    n, ns, most, width_latent,
    feat, weights_any, gains, biases, latent_wide, targets, count,
    tokens_out,
    first, second, raw, taps, slab_out, slab_in, tok_out, tok_in,
    raw_sem, block_send, block_recv, up_send, up_recv, down_send, down_recv,
    slab_send, slab_recv, tok_send, tok_recv,
):
    t = lax.axis_index("tm")
    s = lax.axis_index("space")
    me = t * ns + s
    owners = n * ns
    frames, rows, cols, width = feat.shape
    cells = frames * rows * cols
    out = weights_any.shape[1]
    pack = max(1, LANES // out)
    part = cells // pack
    step = jnp.where(t < n // 2, 1, -1)

    barrier = pltpu.get_barrier_semaphore()

    def greet(d, carry):
        o = (me + d) % owners
        pl.semaphore_signal(
            barrier, inc=1, device_id={"tm": o // ns, "space": o % ns}, device_id_type=MESH
        )
        return carry

    lax.fori_loop(1, owners, greet, 0)
    weight_copy = pltpu.make_async_copy(weights_any, raw, raw_sem)
    weight_copy.start()

    for buf in (first, second):
        buf[0:2] = jnp.zeros((2,) + buf.shape[1:], buf.dtype)

        @pl.when(s == 0)
        def _():
            buf[:, 0:1] = jnp.zeros((buf.shape[0], 1) + buf.shape[2:], buf.dtype)

        @pl.when(s == ns - 1)
        def _():
            buf[:, rows + 1 : rows + 2] = jnp.zeros((buf.shape[0], 1) + buf.shape[2:], buf.dtype)

    inputs = feat[...].reshape(cells, width).astype(jnp.float32)

    def keep(buf, active):
        buf[pl.ds(2 + frames * t, frames), 1 : rows + 1] = active.astype(jnp.bfloat16).reshape(
            frames, rows, cols, width
        )

    def block_copy(buf, layer, source, target):
        span = buf.at[pl.ds(2 + frames * source, frames), pl.ds(1, rows)]
        return pltpu.make_async_remote_copy(
            src_ref=span, dst_ref=span,
            send_sem=block_send.at[layer, target], recv_sem=block_recv.at[layer, source],
            device_id={"tm": target}, device_id_type=MESH,
        )

    def up_copy(buf, layer, source, target, side):
        return pltpu.make_async_remote_copy(
            src_ref=buf.at[pl.ds(2 + frames * source, frames), pl.ds(1, 1)],
            dst_ref=buf.at[pl.ds(2 + frames * source, frames), pl.ds(rows + 1, 1)],
            send_sem=up_send.at[layer, target], recv_sem=up_recv.at[layer, source],
            device_id={"tm": target, "space": side}, device_id_type=MESH,
        )

    def down_copy(buf, layer, source, target, side):
        return pltpu.make_async_remote_copy(
            src_ref=buf.at[pl.ds(2 + frames * source, frames), pl.ds(rows, 1)],
            dst_ref=buf.at[pl.ds(2 + frames * source, frames), pl.ds(0, 1)],
            send_sem=down_send.at[layer, target], recv_sem=down_recv.at[layer, source],
            device_id={"tm": target, "space": side}, device_id_type=MESH,
        )

    def slab_copy(layer, source, target):
        return pltpu.make_async_remote_copy(
            src_ref=slab_out.at[layer, target], dst_ref=slab_in.at[layer, source],
            send_sem=slab_send.at[layer, target], recv_sem=slab_recv.at[layer, source],
            device_id={"tm": target}, device_id_type=MESH,
        )

    def spread(buf, layer):
        def send(k, carry):
            target = (t + k * step + n) % n

            @pl.when(k > 0)
            def _():
                block_copy(buf, layer, t, target).start()

            @pl.when(s > 0)
            def _():
                up_copy(buf, layer, t, target, s - 1).start()

            @pl.when(s < ns - 1)
            def _():
                down_copy(buf, layer, t, target, s + 1).start()

            return carry

        lax.fori_loop(0, n, send, 0)

    def spread_sent(buf, layer):
        def sent(k, carry):
            target = (t + k * step + n) % n

            @pl.when(k > 0)
            def _():
                block_copy(buf, layer, t, target).wait_send()
                slab_copy(layer, t, target).wait_send()

            @pl.when(s > 0)
            def _():
                up_copy(buf, layer, t, target, s - 1).wait_send()

            @pl.when(s < ns - 1)
            def _():
                down_copy(buf, layer, t, target, s + 1).wait_send()

            return carry

        lax.fori_loop(0, n, sent, 0)

    def arrive(buf, layer, c):
        @pl.when(c != t)
        def _():
            block_copy(buf, layer, c, c).wait_recv()

        @pl.when(s < ns - 1)
        def _():
            up_copy(buf, layer, c, c, s + 1).wait_recv()

        @pl.when(s > 0)
        def _():
            down_copy(buf, layer, c, c, s - 1).wait_recv()

    column = lax.broadcasted_iota(jnp.int32, (cells, 1), 0) % cols

    def convolve(buf, layer):
        def place(b):
            return ((b - t) * step + n) % n

        def one(k, carry):
            b = (t + k * step + n) % n
            here = place(b)

            @pl.when((b == n - 1) | (place((b + 1) % n) > here))
            def _():
                arrive(buf, layer, b)

            @pl.when((b > 0) & (place((b + n - 1) % n) > here))
            def _():
                arrive(buf, layer, (b + n - 1) % n)

            total = jnp.zeros((cells, 3 * out), jnp.float32)
            for a in range(3):
                for r in range(3):
                    block = buf[pl.ds(frames * b + a, frames), r : r + rows]
                    total = total + lax.dot_general(
                        block.reshape(cells, width), taps[layer, 3 * a + r],
                        (((1,), (1,)), ((), ())), preferred_element_type=jnp.float32,
                    )
            left = jnp.where(column == 0, 0.0, pltpu.roll(total[:, :out], 1, 0))
            right = jnp.where(column == cols - 1, 0.0, pltpu.roll(total[:, 2 * out :], cells - 1, 0))
            summed = (left + total[:, out : 2 * out] + right).astype(jnp.bfloat16)
            packed = jnp.concatenate(
                [summed[j * part : (j + 1) * part] for j in range(pack)], axis=1
            )

            @pl.when(b == t)
            def _():
                slab_in[layer, pl.ds(t, 1)] = packed[None]

            @pl.when(b != t)
            def _():
                slab_out[layer, pl.ds(b, 1)] = packed[None]
                slab_copy(layer, t, b).start()

            return carry

        lax.fori_loop(0, n, one, 0)

        def came(k, carry):
            slab_copy(layer, (t + k) % n, (t + k) % n).wait_recv()
            return carry

        lax.fori_loop(1, n, came, 0)
        pieces = [slab_in[layer, q].astype(jnp.float32) for q in range(n)]
        hidden = jnp.concatenate(
            [
                jnp.concatenate([piece[:, j * out : (j + 1) * out] for piece in pieces], axis=1)
                for j in range(pack)
            ],
            axis=0,
        )
        return hidden + biases[layer : layer + 1]

    keep(first, norm_silu(inputs, gains[0:1]))
    pl.semaphore_wait(barrier, owners - 1)
    spread(first, 0)
    weight_copy.wait()
    for layer in range(2):
        for tap in range(27):
            group, e = tap // 3, tap % 3
            taps[layer, group, e * out : (e + 1) * out] = raw[layer, :, tap, :]
    hidden = convolve(first, 0)
    keep(second, norm_silu(hidden, gains[1:2]))
    spread(second, 1)
    hidden = convolve(second, 1)
    merged = feat[...].reshape(cells, width).astype(jnp.float32) + hidden
    active = norm_silu(merged, gains[2:3]).astype(jnp.bfloat16)
    latent = jnp.dot(active, latent_wide[...], preferred_element_type=jnp.float32)
    cell = lax.broadcasted_iota(jnp.int32, (cells, LANES), 0)
    lane = lax.broadcasted_iota(jnp.int32, (cells, LANES), 1)
    corner = (cell // cols % 2) * 2 + cell % 2
    alive = (t * frames + cell // (rows * cols) < count[0]) & (corner == 0)
    flagged = jnp.where((lane == 4 * width_latent) & alive, 1.0, 0.0)
    patches = jnp.where(lane // width_latent == corner, latent, flagged).astype(jnp.bfloat16)
    slots = lax.broadcasted_iota(jnp.int32, (owners * SUBLANES, cells), 0)
    placing = jnp.where(slots == targets[...], 1.0, 0.0).astype(jnp.bfloat16)
    outgoing = jnp.dot(placing, patches, preferred_element_type=jnp.float32).astype(jnp.bfloat16)
    tok_out[...] = outgoing.reshape(owners, SUBLANES, LANES)
    tok_in[pl.ds(me, 1)] = tok_out[pl.ds(me, 1)]

    def tok_copy(source, target):
        return pltpu.make_async_remote_copy(
            src_ref=tok_out.at[target], dst_ref=tok_in.at[source],
            send_sem=tok_send.at[target], recv_sem=tok_recv.at[source],
            device_id={"tm": target // ns, "space": target % ns}, device_id_type=MESH,
        )

    def tok_start(d, carry):
        tok_copy(me, (me + d) % owners).start()
        return carry

    def tok_wait(d, carry):
        o = (me + d) % owners
        tok_copy(o, o).wait_recv()
        return carry

    def tok_sent(d, carry):
        tok_copy(me, (me + d) % owners).wait_send()
        return carry

    lax.fori_loop(1, owners, tok_start, 0)
    spread_sent(first, 0)
    spread_sent(second, 1)
    lax.fori_loop(1, owners, tok_wait, 0)
    row = lax.broadcasted_iota(jnp.int32, (owners * most, owners * SUBLANES), 0)
    held = lax.broadcasted_iota(jnp.int32, (owners * most, owners * SUBLANES), 1)
    inner = held % SUBLANES
    chosen = (row == held // SUBLANES * most + inner) & (inner < most)
    tokens_out[...] = jnp.dot(
        jnp.where(chosen, 1.0, 0.0).astype(jnp.bfloat16),
        tok_in[...].reshape(owners * SUBLANES, LANES),
        preferred_element_type=jnp.float32,
    ).astype(jnp.bfloat16)
    lax.fori_loop(1, owners, tok_sent, 0)


def shards(
    features,
    frame_counts,
    routes,
    norm_gains,
    conv_weights,
    conv_biases,
    latent_weight,
    embed_weight,
    embed_bias,
):
    feat = features[0]
    frames, rows, cols, width = feat.shape
    cells = frames * rows * cols
    n, ns = lax.axis_size("tm"), lax.axis_size("space")
    owners = n * ns
    out = conv_weights.shape[1]
    pack = max(1, LANES // out)
    latents = latent_weight.shape[1]
    tok_count = routes.shape[1]
    most = (tok_count + owners - 1) // owners + 1
    destinations = routes[0, :, 0]
    positions = jnp.arange(tok_count, dtype=jnp.int32)
    before = positions[:, None] > positions[None, :]
    ranks = jnp.sum(
        ((destinations[:, None] == destinations[None, :]) & before).astype(jnp.int32), axis=1
    )
    slots = (destinations * SUBLANES + ranks).reshape(frames, rows // 2, 1, cols // 2, 1)
    targets = jnp.broadcast_to(slots, (frames, rows // 2, 2, cols // 2, 2)).reshape(1, cells)
    latent_wide = jnp.pad(
        jnp.concatenate([latent_weight] * 4, axis=1), ((0, 0), (0, LANES - 4 * latents))
    )
    vmem = pl.BlockSpec(memory_space=pltpu.VMEM)
    dma = pltpu.SemaphoreType.DMA
    field = pltpu.VMEM((n * frames + 2, rows + 2, cols, width), jnp.bfloat16)
    slab = pltpu.VMEM((2, n, cells // pack, pack * out), jnp.bfloat16)
    tok = pltpu.VMEM((owners, SUBLANES, LANES), jnp.bfloat16)
    tokens = pl.pallas_call(
        functools.partial(encoder, n, ns, most, latents),
        out_shape=jax.ShapeDtypeStruct((owners * most, LANES), jnp.bfloat16),
        in_specs=[vmem, pl.BlockSpec(memory_space=pl.ANY), vmem, vmem, vmem, vmem,
                  pl.BlockSpec(memory_space=pltpu.SMEM)],
        out_specs=vmem,
        scratch_shapes=[
            field, field,
            pltpu.VMEM(conv_weights.shape, jnp.bfloat16),
            pltpu.VMEM((2, 9, 3 * out, width), jnp.bfloat16),
            slab, slab, tok, tok,
            dma,
            dma((2, n)), dma((2, n)), dma((2, n)), dma((2, n)), dma((2, n)), dma((2, n)),
            dma((2, n)), dma((2, n)), dma((owners,)), dma((owners,)),
        ],
        compiler_params=pltpu.CompilerParams(collective_id=0, has_side_effects=True),
    )(feat, conv_weights, norm_gains, conv_biases, latent_wide, targets, frame_counts)
    channels = 4 * latents
    projected = (
        jnp.dot(tokens[:, :channels], embed_weight, preferred_element_type=jnp.float32) + embed_bias
    ) * tokens[:, channels : channels + 1].astype(jnp.float32)
    return projected.astype(jnp.bfloat16)[None]


def solution(mesh):
    return jax.shard_map(
        shards,
        mesh=mesh,
        in_specs=(
            P(("groups", "clip"), "tm", "space", None, None),
            P(("groups", "clip")),
            P(("groups", "clip"), ("tm", "space"), None),
            P(),
            P(None, "tm", None, None),
            P(),
            P(),
            P(),
            P(),
        ),
        out_specs=P(("groups", "clip"), ("tm", "space"), None),
        check_vma=False,
    )
```

```python
import functools

import jax
import jax.numpy as jnp
from jax import lax
from jax.experimental import pallas as pl
from jax.experimental.pallas import tpu as pltpu
from jax.sharding import PartitionSpec as P

MESH = pl.DeviceIdType.MESH
LANES = 128
SUBLANES = 16


def norm_silu(values, gain):
    scale = lax.rsqrt(jnp.mean(values * values, axis=-1, keepdims=True) + 1e-06)
    scaled = values * scale * gain
    return scaled / (1.0 + jnp.exp(-scaled))


def encoder(
    n, ns, most, width_latent,
    feat, weights_any, gains, biases, latent_rows, owner_of, count,
    tokens_out,
    first, second, taps, placing, slab_out, slab_in, tok_out, tok_in,
    raw_sem, block_send, block_recv, up_send, up_recv, down_send, down_recv,
    slab_send, slab_recv, tok_send, tok_recv,
):
    t = lax.axis_index("tm")
    s = lax.axis_index("space")
    me = t * ns + s
    owners = n * ns
    frames, rows, cols, width = feat.shape
    cells = frames * rows * cols
    out = weights_any.shape[2] // 3
    pack = max(1, LANES // out)
    part = cells // pack
    step = jnp.where(t < n // 2, 1, -1)

    barrier = pltpu.get_barrier_semaphore()

    def greet(d, carry):
        o = (me + d) % owners
        pl.semaphore_signal(
            barrier, inc=1, device_id={"tm": o // ns, "space": o % ns}, device_id_type=MESH
        )
        return carry

    lax.fori_loop(1, owners, greet, 0)
    weight_copy = pltpu.make_async_copy(weights_any, taps, raw_sem)
    weight_copy.start()

    for buf in (first, second):
        buf[0:2] = jnp.zeros((2,) + buf.shape[1:], buf.dtype)

        @pl.when(s == 0)
        def _():
            buf[:, 0:1] = jnp.zeros((buf.shape[0], 1) + buf.shape[2:], buf.dtype)

        @pl.when(s == ns - 1)
        def _():
            buf[:, rows + 1 : rows + 2] = jnp.zeros((buf.shape[0], 1) + buf.shape[2:], buf.dtype)

    inputs = feat[...].reshape(cells, width).astype(jnp.float32)

    def keep(buf, active):
        buf[pl.ds(2 + frames * t, frames), 1 : rows + 1] = active.astype(jnp.bfloat16).reshape(
            frames, rows, cols, width
        )

    def block_copy(buf, layer, source, target):
        span = buf.at[pl.ds(2 + frames * source, frames), pl.ds(1, rows)]
        return pltpu.make_async_remote_copy(
            src_ref=span, dst_ref=span,
            send_sem=block_send.at[layer, target], recv_sem=block_recv.at[layer, source],
            device_id={"tm": target}, device_id_type=MESH,
        )

    def up_copy(buf, layer, source, target, side):
        return pltpu.make_async_remote_copy(
            src_ref=buf.at[pl.ds(2 + frames * source, frames), pl.ds(1, 1)],
            dst_ref=buf.at[pl.ds(2 + frames * source, frames), pl.ds(rows + 1, 1)],
            send_sem=up_send.at[layer, target], recv_sem=up_recv.at[layer, source],
            device_id={"tm": target, "space": side}, device_id_type=MESH,
        )

    def down_copy(buf, layer, source, target, side):
        return pltpu.make_async_remote_copy(
            src_ref=buf.at[pl.ds(2 + frames * source, frames), pl.ds(rows, 1)],
            dst_ref=buf.at[pl.ds(2 + frames * source, frames), pl.ds(0, 1)],
            send_sem=down_send.at[layer, target], recv_sem=down_recv.at[layer, source],
            device_id={"tm": target, "space": side}, device_id_type=MESH,
        )

    def slab_copy(layer, source, target):
        return pltpu.make_async_remote_copy(
            src_ref=slab_out.at[layer, target], dst_ref=slab_in.at[layer, source],
            send_sem=slab_send.at[layer, target], recv_sem=slab_recv.at[layer, source],
            device_id={"tm": target}, device_id_type=MESH,
        )

    def spread(buf, layer):
        def send(k, carry):
            target = (t + k * step + n) % n

            @pl.when(k > 0)
            def _():
                block_copy(buf, layer, t, target).start()

            @pl.when(s > 0)
            def _():
                up_copy(buf, layer, t, target, s - 1).start()

            @pl.when(s < ns - 1)
            def _():
                down_copy(buf, layer, t, target, s + 1).start()

            return carry

        lax.fori_loop(0, n, send, 0)

    def spread_sent(buf, layer):
        def sent(k, carry):
            target = (t + k * step + n) % n

            @pl.when(k > 0)
            def _():
                block_copy(buf, layer, t, target).wait_send()
                slab_copy(layer, t, target).wait_send()

            @pl.when(s > 0)
            def _():
                up_copy(buf, layer, t, target, s - 1).wait_send()

            @pl.when(s < ns - 1)
            def _():
                down_copy(buf, layer, t, target, s + 1).wait_send()

            return carry

        lax.fori_loop(0, n, sent, 0)

    def arrive(buf, layer, c):
        @pl.when(c != t)
        def _():
            block_copy(buf, layer, c, c).wait_recv()

        @pl.when(s < ns - 1)
        def _():
            up_copy(buf, layer, c, c, s + 1).wait_recv()

        @pl.when(s > 0)
        def _():
            down_copy(buf, layer, c, c, s - 1).wait_recv()

    column = lax.broadcasted_iota(jnp.int32, (cells, 1), 0) % cols

    def convolve(buf, layer):
        def place(b):
            return ((b - t) * step + n) % n

        def one(k, carry):
            b = (t + k * step + n) % n
            here = place(b)

            @pl.when((b == n - 1) | (place((b + 1) % n) > here))
            def _():
                arrive(buf, layer, b)

            @pl.when((b > 0) & (place((b + n - 1) % n) > here))
            def _():
                arrive(buf, layer, (b + n - 1) % n)

            total = jnp.zeros((cells, 3 * out), jnp.float32)
            for a in range(3):
                for r in range(3):
                    block = buf[pl.ds(frames * b + a, frames), r : r + rows]
                    total = total + lax.dot_general(
                        block.reshape(cells, width), taps[layer, 3 * a + r],
                        (((1,), (1,)), ((), ())), preferred_element_type=jnp.float32,
                    )
            left = jnp.where(column == 0, 0.0, pltpu.roll(total[:, :out], 1, 0))
            right = jnp.where(column == cols - 1, 0.0, pltpu.roll(total[:, 2 * out :], cells - 1, 0))
            summed = (left + total[:, out : 2 * out] + right).astype(jnp.bfloat16)
            packed = jnp.concatenate(
                [summed[j * part : (j + 1) * part] for j in range(pack)], axis=1
            )

            @pl.when(b == t)
            def _():
                slab_in[layer, pl.ds(t, 1)] = packed[None]

            @pl.when(b != t)
            def _():
                slab_out[layer, pl.ds(b, 1)] = packed[None]
                slab_copy(layer, t, b).start()

            return carry

        lax.fori_loop(0, n, one, 0)

        def came(k, carry):
            slab_copy(layer, (t + k) % n, (t + k) % n).wait_recv()
            return carry

        lax.fori_loop(1, n, came, 0)
        pieces = [slab_in[layer, q].astype(jnp.float32) for q in range(n)]
        hidden = jnp.concatenate(
            [
                jnp.concatenate([piece[:, j * out : (j + 1) * out] for piece in pieces], axis=1)
                for j in range(pack)
            ],
            axis=0,
        )
        return hidden + biases[layer : layer + 1]

    keep(first, norm_silu(inputs, gains[0:1]))
    pl.semaphore_wait(barrier, owners - 1)
    spread(first, 0)
    toks = owner_of.shape[1]
    before = lax.broadcasted_iota(jnp.int32, (toks, toks), 0)
    after = lax.broadcasted_iota(jnp.int32, (toks, toks), 1)
    owner = owner_of[...]
    owner_column = jnp.sum(jnp.where(before == after, owner, 0), axis=1, keepdims=True)
    same = (owner_column == owner) & (before < after)
    rank = jnp.sum(jnp.where(same, 1, 0), axis=0, keepdims=True)
    slots = lax.broadcasted_iota(jnp.int32, (owners * SUBLANES, toks), 0)
    placing[...] = jnp.where(slots == owner * SUBLANES + rank, 1.0, 0.0).astype(jnp.bfloat16)
    weight_copy.wait()
    hidden = convolve(first, 0)
    keep(second, norm_silu(hidden, gains[1:2]))
    spread(second, 1)
    hidden = convolve(second, 1)
    merged = feat[...].reshape(cells, width).astype(jnp.float32) + hidden
    active = norm_silu(merged, gains[2:3]).astype(jnp.bfloat16)
    rest = jnp.zeros((LANES - 4 * width_latent, width), jnp.bfloat16)
    latent_wide = jnp.concatenate([latent_rows[...]] * 4 + [rest], axis=0)
    latent = lax.dot_general(
        active, latent_wide, (((1,), (1,)), ((), ())), preferred_element_type=jnp.float32
    )
    cell = lax.broadcasted_iota(jnp.int32, (cells, LANES), 0)
    lane = lax.broadcasted_iota(jnp.int32, (cells, LANES), 1)
    corner = (cell // cols % 2) * 2 + cell % 2
    alive = (t * frames + cell // (rows * cols) < count[0]) & (corner == 0)
    flagged = jnp.where((lane == 4 * width_latent) & alive, 1.0, 0.0)
    patches = jnp.where(lane // width_latent == corner, latent, flagged).astype(jnp.bfloat16)
    spot = lax.broadcasted_iota(jnp.int32, (toks, cells), 1)
    patch = (spot // (2 * cols)) * (cols // 2) + spot % cols // 2
    mine = patch == lax.broadcasted_iota(jnp.int32, (toks, cells), 0)
    patches = jnp.dot(
        jnp.where(mine, 1.0, 0.0).astype(jnp.bfloat16), patches, preferred_element_type=jnp.float32
    ).astype(jnp.bfloat16)
    outgoing = jnp.dot(
        placing[...], patches, preferred_element_type=jnp.float32
    ).astype(jnp.bfloat16)
    tok_out[...] = outgoing.reshape(owners, SUBLANES, LANES)
    tok_in[pl.ds(me, 1)] = tok_out[pl.ds(me, 1)]

    def tok_copy(source, target):
        return pltpu.make_async_remote_copy(
            src_ref=tok_out.at[target], dst_ref=tok_in.at[source],
            send_sem=tok_send.at[target], recv_sem=tok_recv.at[source],
            device_id={"tm": target // ns, "space": target % ns}, device_id_type=MESH,
        )

    def tok_start(d, carry):
        tok_copy(me, (me + d) % owners).start()
        return carry

    def tok_wait(d, carry):
        o = (me + d) % owners
        tok_copy(o, o).wait_recv()
        return carry

    def tok_sent(d, carry):
        tok_copy(me, (me + d) % owners).wait_send()
        return carry

    lax.fori_loop(1, owners, tok_start, 0)
    spread_sent(first, 0)
    spread_sent(second, 1)
    lax.fori_loop(1, owners, tok_wait, 0)
    row = lax.broadcasted_iota(jnp.int32, (owners * most, owners * SUBLANES), 0)
    held = lax.broadcasted_iota(jnp.int32, (owners * most, owners * SUBLANES), 1)
    inner = held % SUBLANES
    chosen = (row == held // SUBLANES * most + inner) & (inner < most)
    tokens_out[...] = jnp.dot(
        jnp.where(chosen, 1.0, 0.0).astype(jnp.bfloat16),
        tok_in[...].reshape(owners * SUBLANES, LANES),
        preferred_element_type=jnp.float32,
    ).astype(jnp.bfloat16)
    lax.fori_loop(1, owners, tok_sent, 0)


def embedder(channels, tokens, weight, bias, packed):
    held = tokens[...]
    projected = jnp.dot(held[:, :channels], weight[...], preferred_element_type=jnp.float32)
    flags = held[:, channels : channels + 1].astype(jnp.float32)
    packed[...] = ((projected + bias[...]) * flags).astype(jnp.bfloat16)


def shards(
    features,
    frame_counts,
    routes,
    norm_gains,
    conv_weights,
    conv_biases,
    latent_weight,
    embed_weight,
    embed_bias,
):
    feat = features[0]
    frames, rows, cols, width = feat.shape
    cells = frames * rows * cols
    n, ns = lax.axis_size("tm"), lax.axis_size("space")
    owners = n * ns
    out = conv_weights.shape[1]
    pack = max(1, LANES // out)
    latents = latent_weight.shape[1]
    tok_count = routes.shape[1]
    most = (tok_count + owners - 1) // owners + 1
    vmem = pl.BlockSpec(memory_space=pltpu.VMEM)
    dma = pltpu.SemaphoreType.DMA
    field = pltpu.VMEM((n * frames + 2, rows + 2, cols, width), jnp.bfloat16)
    slab = pltpu.VMEM((2, n, cells // pack, pack * out), jnp.bfloat16)
    tok = pltpu.VMEM((owners, SUBLANES, LANES), jnp.bfloat16)
    tokens = pl.pallas_call(
        functools.partial(encoder, n, ns, most, latents),
        out_shape=jax.ShapeDtypeStruct((owners * most, LANES), jnp.bfloat16),
        in_specs=[vmem, pl.BlockSpec(memory_space=pl.ANY), vmem, vmem, vmem, vmem,
                  pl.BlockSpec(memory_space=pltpu.SMEM)],
        out_specs=vmem,
        scratch_shapes=[
            field, field,
            pltpu.VMEM((2, 9, 3 * out, width), jnp.bfloat16),
            pltpu.VMEM((owners * SUBLANES, tok_count), jnp.bfloat16),
            slab, slab, tok, tok,
            dma,
            dma((2, n)), dma((2, n)), dma((2, n)), dma((2, n)), dma((2, n)), dma((2, n)),
            dma((2, n)), dma((2, n)), dma((owners,)), dma((owners,)),
        ],
        compiler_params=pltpu.CompilerParams(collective_id=0, has_side_effects=True),
    )(
        feat,
        conv_weights.transpose(0, 2, 1, 3).reshape(2, 9, 3 * out, width),
        norm_gains,
        conv_biases,
        latent_weight.T,
        routes.reshape(1, tok_count),
        frame_counts,
    )
    channels = 4 * latents
    embed = embed_weight.shape[1]
    chunk = embed // 3 if embed % (3 * LANES) == 0 else embed
    packed = pl.pallas_call(
        functools.partial(embedder, channels),
        grid=(embed // chunk,),
        out_shape=jax.ShapeDtypeStruct((owners * most, embed), jnp.bfloat16),
        in_specs=[
            pl.BlockSpec((owners * most, LANES), lambda i: (0, 0)),
            pl.BlockSpec((channels, chunk), lambda i: (0, i)),
            pl.BlockSpec((1, chunk), lambda i: (0, i)),
        ],
        out_specs=pl.BlockSpec((owners * most, chunk), lambda i: (0, i)),
    )(tokens, embed_weight, embed_bias.reshape(1, embed))
    return packed[None]


def solution(mesh):
    return jax.shard_map(
        shards,
        mesh=mesh,
        in_specs=(
            P(("groups", "clip"), "tm", "space", None, None),
            P(("groups", "clip")),
            P(("groups", "clip"), ("tm", "space"), None),
            P(),
            P(None, "tm", None, None),
            P(),
            P(),
            P(),
            P(),
        ),
        out_specs=P(("groups", "clip"), ("tm", "space"), None),
        check_vma=False,
    )
```

```python
import functools

import jax
import jax.numpy as jnp
from jax import lax
from jax.experimental import pallas as pl
from jax.experimental.pallas import tpu as pltpu
from jax.sharding import PartitionSpec as P

MESH = pl.DeviceIdType.MESH
LANES = 128
SUBLANES = 16
CUTS = 2


def norm_silu(values, gain):
    scale = lax.rsqrt(jnp.mean(values * values, axis=-1, keepdims=True) + 1e-06)
    scaled = values * scale * gain
    return scaled / (1.0 + jnp.exp(-scaled))


def encoder(
    n, ns, most, width_latent,
    feat, weights_any, gains, biases, latent_rows, owner_of, count,
    tokens_out,
    first, second, taps, placing, slab_out, slab_in, tok_out, tok_in,
    raw_sem, block_send, block_recv, up_send, up_recv, down_send, down_recv,
    slab_send, slab_recv, tok_send, tok_recv,
):
    t = lax.axis_index("tm")
    s = lax.axis_index("space")
    me = t * ns + s
    owners = n * ns
    frames, rows, cols, width = feat.shape
    cells = frames * rows * cols
    out = weights_any.shape[2] // 3
    cuts = block_recv.shape[2]
    size = frames // cuts
    pack = max(1, LANES // out)
    part = cells // pack

    barrier = pltpu.get_barrier_semaphore()

    def greet(d, carry):
        o = (me + d) % owners
        pl.semaphore_signal(
            barrier, inc=1, device_id={"tm": o // ns, "space": o % ns}, device_id_type=MESH
        )
        return carry

    lax.fori_loop(1, owners, greet, 0)
    weight_copy = pltpu.make_async_copy(weights_any, taps, raw_sem)
    weight_copy.start()

    for buf in (first, second):
        buf[0:2] = jnp.zeros((2,) + buf.shape[1:], buf.dtype)

        @pl.when(s == 0)
        def _():
            buf[:, 0:1] = jnp.zeros((buf.shape[0], 1) + buf.shape[2:], buf.dtype)

        @pl.when(s == ns - 1)
        def _():
            buf[:, rows + 1 : rows + 2] = jnp.zeros((buf.shape[0], 1) + buf.shape[2:], buf.dtype)

    inputs = feat[...].reshape(cells, width).astype(jnp.float32)

    def keep(buf, active):
        buf[pl.ds(2 + frames * t, frames), 1 : rows + 1] = active.astype(jnp.bfloat16).reshape(
            frames, rows, cols, width
        )

    def block_copy(buf, layer, c, f, way):
        span = buf.at[pl.ds(2 + frames * c + size * f, size), pl.ds(1, rows)]
        return pltpu.make_async_remote_copy(
            src_ref=span, dst_ref=span,
            send_sem=block_send.at[layer, way, c, f], recv_sem=block_recv.at[layer, c, f],
            device_id={"tm": (t + 1 - 2 * way + n) % n}, device_id_type=MESH,
        )

    def up_copy(buf, layer, c, f):
        return pltpu.make_async_remote_copy(
            src_ref=buf.at[pl.ds(2 + frames * c + size * f, size), pl.ds(1, 1)],
            dst_ref=buf.at[pl.ds(2 + frames * c + size * f, size), pl.ds(rows + 1, 1)],
            send_sem=up_send.at[layer, c, f], recv_sem=up_recv.at[layer, c, f],
            device_id={"space": (s + ns - 1) % ns}, device_id_type=MESH,
        )

    def down_copy(buf, layer, c, f):
        return pltpu.make_async_remote_copy(
            src_ref=buf.at[pl.ds(2 + frames * c + size * f, size), pl.ds(rows, 1)],
            dst_ref=buf.at[pl.ds(2 + frames * c + size * f, size), pl.ds(0, 1)],
            send_sem=down_send.at[layer, c, f], recv_sem=down_recv.at[layer, c, f],
            device_id={"space": (s + 1) % ns}, device_id_type=MESH,
        )

    def slab_copy(layer, source, target):
        return pltpu.make_async_remote_copy(
            src_ref=slab_out.at[layer, target], dst_ref=slab_in.at[layer, source],
            send_sem=slab_send.at[layer, target], recv_sem=slab_recv.at[layer, source],
            device_id={"tm": target}, device_id_type=MESH,
        )

    def outward(buf, layer, c, f, act):
        pl.when((c <= t) & (t < n - 1))(lambda: act(block_copy(buf, layer, c, f, 0)))
        pl.when((c >= t) & (t > 0))(lambda: act(block_copy(buf, layer, c, f, 1)))
        pl.when(s > 0)(lambda: act(up_copy(buf, layer, c, f)))
        pl.when(s < ns - 1)(lambda: act(down_copy(buf, layer, c, f)))

    def spread(buf, layer):
        for f in range(cuts):
            outward(buf, layer, t, f, lambda copy: copy.start())

    def spread_sent(buf, layer):
        def sent(c, carry):
            for f in range(cuts):
                outward(buf, layer, c, f, lambda copy: copy.wait_send())

            @pl.when(c != t)
            def _():
                slab_copy(layer, t, c).wait_send()

            return carry

        lax.fori_loop(0, n, sent, 0)

    def handle(buf, layer, c, f):
        block_copy(buf, layer, c, f, 0).wait_recv()
        outward(buf, layer, c, f, lambda copy: copy.start())

    def rims(buf, layer, c):
        for f in range(cuts):
            pl.when(s < ns - 1)(lambda: up_copy(buf, layer, c, f).wait_recv())
            pl.when(s > 0)(lambda: down_copy(buf, layer, c, f).wait_recv())

    column = lax.broadcasted_iota(jnp.int32, (cells, 1), 0) % cols

    def convolve(buf, layer):
        def one(b):
            total = jnp.zeros((cells, 3 * out), jnp.float32)
            for a in range(3):
                for r in range(3):
                    block = buf[pl.ds(frames * b + a, frames), r : r + rows]
                    total = total + lax.dot_general(
                        block.reshape(cells, width), taps[layer, 3 * a + r],
                        (((1,), (1,)), ((), ())), preferred_element_type=jnp.float32,
                    )
            left = jnp.where(column == 0, 0.0, pltpu.roll(total[:, :out], 1, 0))
            right = jnp.where(column == cols - 1, 0.0, pltpu.roll(total[:, 2 * out :], cells - 1, 0))
            summed = (left + total[:, out : 2 * out] + right).astype(jnp.bfloat16)
            packed = jnp.concatenate(
                [summed[j * part : (j + 1) * part] for j in range(pack)], axis=1
            )

            @pl.when(b == t)
            def _():
                slab_in[layer, pl.ds(t, 1)] = packed[None]

            @pl.when(b != t)
            def _():
                slab_out[layer, pl.ds(b, 1)] = packed[None]
                slab_copy(layer, t, b).start()

        def ring(d, carry):
            low, high = t - d, t + d
            is_low, is_high = low >= 0, high < n
            for f in range(cuts):
                pl.when(is_low)(lambda: handle(buf, layer, (low + n) % n, f))
                pl.when(is_high)(lambda: handle(buf, layer, high % n, f))
            pl.when(d == 1)(lambda: rims(buf, layer, t))
            pl.when(is_low)(lambda: rims(buf, layer, (low + n) % n))
            pl.when(is_high)(lambda: rims(buf, layer, high % n))

            def ready(i, carry):
                b = jnp.where(i == 0, low + 1, high)
                pl.when((b >= 0) & (b < n))(lambda: one((b + n) % n))
                return carry

            lax.fori_loop(0, 2, ready, 0)
            return carry

        lax.fori_loop(1, n + 1, ring, 0)

        def came(k, carry):
            slab_copy(layer, (t + k) % n, (t + k) % n).wait_recv()
            return carry

        lax.fori_loop(1, n, came, 0)
        pieces = [slab_in[layer, q].astype(jnp.float32) for q in range(n)]
        hidden = jnp.concatenate(
            [
                jnp.concatenate([piece[:, j * out : (j + 1) * out] for piece in pieces], axis=1)
                for j in range(pack)
            ],
            axis=0,
        )
        return hidden + biases[layer : layer + 1]

    keep(first, norm_silu(inputs, gains[0:1]))
    toks = owner_of.shape[1]
    before = lax.broadcasted_iota(jnp.int32, (toks, toks), 0)
    after = lax.broadcasted_iota(jnp.int32, (toks, toks), 1)
    owner = owner_of[...]
    owner_column = jnp.sum(jnp.where(before == after, owner, 0), axis=1, keepdims=True)
    same = (owner_column == owner) & (before < after)
    rank = jnp.sum(jnp.where(same, 1, 0), axis=0, keepdims=True)
    slots = lax.broadcasted_iota(jnp.int32, (owners * SUBLANES, toks), 0)
    placing[...] = jnp.where(slots == owner * SUBLANES + rank, 1.0, 0.0).astype(jnp.bfloat16)
    pl.semaphore_wait(barrier, owners - 1)
    spread(first, 0)
    weight_copy.wait()
    hidden = convolve(first, 0)
    keep(second, norm_silu(hidden, gains[1:2]))
    spread(second, 1)
    hidden = convolve(second, 1)
    merged = feat[...].reshape(cells, width).astype(jnp.float32) + hidden
    active = norm_silu(merged, gains[2:3]).astype(jnp.bfloat16)
    rest = jnp.zeros((LANES - 4 * width_latent, width), jnp.bfloat16)
    latent_wide = jnp.concatenate([latent_rows[...]] * 4 + [rest], axis=0)
    latent = lax.dot_general(
        active, latent_wide, (((1,), (1,)), ((), ())), preferred_element_type=jnp.float32
    )
    cell = lax.broadcasted_iota(jnp.int32, (cells, LANES), 0)
    lane = lax.broadcasted_iota(jnp.int32, (cells, LANES), 1)
    corner = (cell // cols % 2) * 2 + cell % 2
    alive = (t * frames + cell // (rows * cols) < count[0]) & (corner == 0)
    flagged = jnp.where((lane == 4 * width_latent) & alive, 1.0, 0.0)
    patches = jnp.where(lane // width_latent == corner, latent, flagged).astype(jnp.bfloat16)
    spot = lax.broadcasted_iota(jnp.int32, (toks, cells), 1)
    patch = (spot // (2 * cols)) * (cols // 2) + spot % cols // 2
    mine = patch == lax.broadcasted_iota(jnp.int32, (toks, cells), 0)
    patches = jnp.dot(
        jnp.where(mine, 1.0, 0.0).astype(jnp.bfloat16), patches, preferred_element_type=jnp.float32
    ).astype(jnp.bfloat16)
    outgoing = jnp.dot(
        placing[...], patches, preferred_element_type=jnp.float32
    ).astype(jnp.bfloat16)
    tok_out[...] = outgoing.reshape(owners, SUBLANES, LANES)
    tok_in[pl.ds(me, 1)] = tok_out[pl.ds(me, 1)]

    def tok_copy(source, target):
        return pltpu.make_async_remote_copy(
            src_ref=tok_out.at[target], dst_ref=tok_in.at[source],
            send_sem=tok_send.at[target], recv_sem=tok_recv.at[source],
            device_id={"tm": target // ns, "space": target % ns}, device_id_type=MESH,
        )

    def tok_start(d, carry):
        tok_copy(me, (me + d) % owners).start()
        return carry

    def tok_wait(d, carry):
        o = (me + d) % owners
        tok_copy(o, o).wait_recv()
        return carry

    def tok_sent(d, carry):
        tok_copy(me, (me + d) % owners).wait_send()
        return carry

    lax.fori_loop(1, owners, tok_start, 0)
    spread_sent(first, 0)
    spread_sent(second, 1)
    lax.fori_loop(1, owners, tok_wait, 0)
    row = lax.broadcasted_iota(jnp.int32, (owners * most, owners * SUBLANES), 0)
    held = lax.broadcasted_iota(jnp.int32, (owners * most, owners * SUBLANES), 1)
    inner = held % SUBLANES
    chosen = (row == held // SUBLANES * most + inner) & (inner < most)
    tokens_out[...] = jnp.dot(
        jnp.where(chosen, 1.0, 0.0).astype(jnp.bfloat16),
        tok_in[...].reshape(owners * SUBLANES, LANES),
        preferred_element_type=jnp.float32,
    ).astype(jnp.bfloat16)
    lax.fori_loop(1, owners, tok_sent, 0)


def embedder(channels, tokens, weight, bias, packed):
    held = tokens[...]
    projected = jnp.dot(held[:, :channels], weight[...], preferred_element_type=jnp.float32)
    flags = held[:, channels : channels + 1].astype(jnp.float32)
    packed[...] = ((projected + bias[...]) * flags).astype(jnp.bfloat16)


def shards(
    features,
    frame_counts,
    routes,
    norm_gains,
    conv_weights,
    conv_biases,
    latent_weight,
    embed_weight,
    embed_bias,
):
    feat = features[0]
    frames, rows, cols, width = feat.shape
    cells = frames * rows * cols
    n, ns = lax.axis_size("tm"), lax.axis_size("space")
    owners = n * ns
    out = conv_weights.shape[1]
    pack = max(1, LANES // out)
    latents = latent_weight.shape[1]
    tok_count = routes.shape[1]
    most = (tok_count + owners - 1) // owners + 1
    vmem = pl.BlockSpec(memory_space=pltpu.VMEM)
    dma = pltpu.SemaphoreType.DMA
    field = pltpu.VMEM((n * frames + 2, rows + 2, cols, width), jnp.bfloat16)
    slab = pltpu.VMEM((2, n, cells // pack, pack * out), jnp.bfloat16)
    cuts = CUTS if frames % CUTS == 0 else 1
    tok = pltpu.VMEM((owners, SUBLANES, LANES), jnp.bfloat16)
    tokens = pl.pallas_call(
        functools.partial(encoder, n, ns, most, latents),
        out_shape=jax.ShapeDtypeStruct((owners * most, LANES), jnp.bfloat16),
        in_specs=[vmem, pl.BlockSpec(memory_space=pl.ANY), vmem, vmem, vmem, vmem,
                  pl.BlockSpec(memory_space=pltpu.SMEM)],
        out_specs=vmem,
        scratch_shapes=[
            field, field,
            pltpu.VMEM((2, 9, 3 * out, width), jnp.bfloat16),
            pltpu.VMEM((owners * SUBLANES, tok_count), jnp.bfloat16),
            slab, slab, tok, tok,
            dma,
            dma((2, 2, n, cuts)), dma((2, n, cuts)), dma((2, n, cuts)), dma((2, n, cuts)),
            dma((2, n, cuts)), dma((2, n, cuts)),
            dma((2, n)), dma((2, n)), dma((owners,)), dma((owners,)),
        ],
        compiler_params=pltpu.CompilerParams(collective_id=0, has_side_effects=True),
    )(
        feat,
        conv_weights.transpose(0, 2, 1, 3).reshape(2, 9, 3 * out, width),
        norm_gains,
        conv_biases,
        latent_weight.T,
        routes.reshape(1, tok_count),
        frame_counts,
    )
    channels = 4 * latents
    embed = embed_weight.shape[1]
    chunk = embed // 1 if embed % (1 * LANES) == 0 else embed
    packed = pl.pallas_call(
        functools.partial(embedder, channels),
        grid=(embed // chunk,),
        out_shape=jax.ShapeDtypeStruct((owners * most, embed), jnp.bfloat16),
        in_specs=[
            pl.BlockSpec((owners * most, LANES), lambda i: (0, 0)),
            pl.BlockSpec((channels, chunk), lambda i: (0, i)),
            pl.BlockSpec((1, chunk), lambda i: (0, i)),
        ],
        out_specs=pl.BlockSpec((owners * most, chunk), lambda i: (0, i)),
    )(tokens, embed_weight, embed_bias.reshape(1, embed))
    return packed[None]


def solution(mesh):
    return jax.shard_map(
        shards,
        mesh=mesh,
        in_specs=(
            P(("groups", "clip"), "tm", "space", None, None),
            P(("groups", "clip")),
            P(("groups", "clip"), ("tm", "space"), None),
            P(),
            P(None, "tm", None, None),
            P(),
            P(),
            P(),
            P(),
        ),
        out_specs=P(("groups", "clip"), ("tm", "space"), None),
        check_vma=False,
    )
```

```python
import functools

import jax
import jax.numpy as jnp
from jax import lax
from jax.experimental import pallas as pl
from jax.experimental.pallas import tpu as pltpu
from jax.sharding import PartitionSpec as P

MESH = pl.DeviceIdType.MESH
LANES = 128
SUBLANES = 16
CUTS = 4


def norm_silu(values, gain):
    scale = lax.rsqrt(jnp.mean(values * values, axis=-1, keepdims=True) + 1e-06)
    scaled = values * scale * gain
    return scaled / (1.0 + jnp.exp(-scaled))


def encoder(
    n, ns, most, width_latent,
    feat, weights_any, gains, biases, latent_rows, owner_of, count,
    tokens_out,
    first, second, taps, placing, slab_out, slab_in, tok_out, tok_in,
    raw_sem, block_send, block_recv, up_send, up_recv, down_send, down_recv,
    slab_send, slab_recv, tok_send, tok_recv,
):
    t = lax.axis_index("tm")
    s = lax.axis_index("space")
    me = t * ns + s
    owners = n * ns
    frames, rows, cols, width = feat.shape
    cells = frames * rows * cols
    out = weights_any.shape[2] // 3
    cuts = block_recv.shape[2]
    size = frames // cuts
    pack = max(1, LANES // out)
    part = cells // pack

    barrier = pltpu.get_barrier_semaphore()

    def greet(d, carry):
        o = (me + d) % owners
        pl.semaphore_signal(
            barrier, inc=1, device_id={"tm": o // ns, "space": o % ns}, device_id_type=MESH
        )
        return carry

    lax.fori_loop(1, owners, greet, 0)
    weight_copy = pltpu.make_async_copy(weights_any, taps, raw_sem)
    weight_copy.start()

    for buf in (first, second):
        buf[0:2] = jnp.zeros((2,) + buf.shape[1:], buf.dtype)

        @pl.when(s == 0)
        def _():
            buf[:, 0:1] = jnp.zeros((buf.shape[0], 1) + buf.shape[2:], buf.dtype)

        @pl.when(s == ns - 1)
        def _():
            buf[:, rows + 1 : rows + 2] = jnp.zeros((buf.shape[0], 1) + buf.shape[2:], buf.dtype)

    inputs = feat[...].reshape(cells, width).astype(jnp.float32)

    def keep(buf, active):
        buf[pl.ds(2 + frames * t, frames), 1 : rows + 1] = active.astype(jnp.bfloat16).reshape(
            frames, rows, cols, width
        )

    def block_copy(buf, layer, c, f, way):
        span = buf.at[pl.ds(2 + frames * c + size * f, size), pl.ds(1, rows)]
        return pltpu.make_async_remote_copy(
            src_ref=span, dst_ref=span,
            send_sem=block_send.at[layer, way, c, f], recv_sem=block_recv.at[layer, c, f],
            device_id={"tm": (t + 1 - 2 * way + n) % n}, device_id_type=MESH,
        )

    def up_copy(buf, layer, c, f):
        return pltpu.make_async_remote_copy(
            src_ref=buf.at[pl.ds(2 + frames * c + size * f, size), pl.ds(1, 1)],
            dst_ref=buf.at[pl.ds(2 + frames * c + size * f, size), pl.ds(rows + 1, 1)],
            send_sem=up_send.at[layer, c, f], recv_sem=up_recv.at[layer, c, f],
            device_id={"space": (s + ns - 1) % ns}, device_id_type=MESH,
        )

    def down_copy(buf, layer, c, f):
        return pltpu.make_async_remote_copy(
            src_ref=buf.at[pl.ds(2 + frames * c + size * f, size), pl.ds(rows, 1)],
            dst_ref=buf.at[pl.ds(2 + frames * c + size * f, size), pl.ds(0, 1)],
            send_sem=down_send.at[layer, c, f], recv_sem=down_recv.at[layer, c, f],
            device_id={"space": (s + 1) % ns}, device_id_type=MESH,
        )

    def slab_copy(layer, source, target):
        return pltpu.make_async_remote_copy(
            src_ref=slab_out.at[layer, target], dst_ref=slab_in.at[layer, source],
            send_sem=slab_send.at[layer, target], recv_sem=slab_recv.at[layer, source],
            device_id={"tm": target}, device_id_type=MESH,
        )

    def outward(buf, layer, c, f, act):
        pl.when((c <= t) & (t < n - 1))(lambda: act(block_copy(buf, layer, c, f, 0)))
        pl.when((c >= t) & (t > 0))(lambda: act(block_copy(buf, layer, c, f, 1)))
        pl.when(s > 0)(lambda: act(up_copy(buf, layer, c, f)))
        pl.when(s < ns - 1)(lambda: act(down_copy(buf, layer, c, f)))

    def spread(buf, layer):
        for f in range(cuts):
            outward(buf, layer, t, f, lambda copy: copy.start())

    def spread_sent(buf, layer):
        def sent(c, carry):
            for f in range(cuts):
                outward(buf, layer, c, f, lambda copy: copy.wait_send())

            @pl.when(c != t)
            def _():
                slab_copy(layer, t, c).wait_send()

            return carry

        lax.fori_loop(0, n, sent, 0)

    def handle(buf, layer, c, f):
        block_copy(buf, layer, c, f, 0).wait_recv()
        outward(buf, layer, c, f, lambda copy: copy.start())

    def rims(buf, layer, c):
        for f in range(cuts):
            pl.when(s < ns - 1)(lambda: up_copy(buf, layer, c, f).wait_recv())
            pl.when(s > 0)(lambda: down_copy(buf, layer, c, f).wait_recv())

    column = lax.broadcasted_iota(jnp.int32, (cells, 1), 0) % cols

    def convolve(buf, layer):
        def one(b):
            total = jnp.zeros((cells, 3 * out), jnp.float32)
            for a in range(3):
                for r in range(3):
                    block = buf[pl.ds(frames * b + a, frames), r : r + rows]
                    total = total + lax.dot_general(
                        block.reshape(cells, width), taps[layer, 3 * a + r],
                        (((1,), (1,)), ((), ())), preferred_element_type=jnp.float32,
                    )
            left = jnp.where(column == 0, 0.0, pltpu.roll(total[:, :out], 1, 0))
            right = jnp.where(column == cols - 1, 0.0, pltpu.roll(total[:, 2 * out :], cells - 1, 0))
            summed = (left + total[:, out : 2 * out] + right).astype(jnp.bfloat16)
            packed = jnp.concatenate(
                [summed[j * part : (j + 1) * part] for j in range(pack)], axis=1
            )

            @pl.when(b == t)
            def _():
                slab_in[layer, pl.ds(t, 1)] = packed[None]

            @pl.when(b != t)
            def _():
                slab_out[layer, pl.ds(b, 1)] = packed[None]
                slab_copy(layer, t, b).start()

        def ring(d, carry):
            low, high = t - d, t + d
            is_low, is_high = low >= 0, high < n
            for f in range(cuts):
                pl.when(is_low)(lambda: handle(buf, layer, (low + n) % n, f))
                pl.when(is_high)(lambda: handle(buf, layer, high % n, f))
            low, high = low + 1, high - 1
            is_low, is_high = (low >= 0) & (low < t), (high < n) & (high > t)
            pl.when(d == 2)(lambda: rims(buf, layer, t))
            pl.when(is_low)(lambda: rims(buf, layer, (low + n) % n))
            pl.when(is_high)(lambda: rims(buf, layer, high % n))

            def ready(i, carry):
                b = jnp.where(i == 0, high, low + 1)
                pl.when((d > 1) & (b >= 0) & (b < n))(lambda: one((b + n) % n))
                return carry

            lax.fori_loop(0, 2, ready, 0)
            return carry

        lax.fori_loop(1, n + 2, ring, 0)

        def came(k, carry):
            slab_copy(layer, (t + k) % n, (t + k) % n).wait_recv()
            return carry

        lax.fori_loop(1, n, came, 0)
        pieces = [slab_in[layer, q].astype(jnp.float32) for q in range(n)]
        hidden = jnp.concatenate(
            [
                jnp.concatenate([piece[:, j * out : (j + 1) * out] for piece in pieces], axis=1)
                for j in range(pack)
            ],
            axis=0,
        )
        return hidden + biases[layer : layer + 1]

    keep(first, norm_silu(inputs, gains[0:1]))
    toks = owner_of.shape[1]
    before = lax.broadcasted_iota(jnp.int32, (toks, toks), 0)
    after = lax.broadcasted_iota(jnp.int32, (toks, toks), 1)
    owner = owner_of[...]
    owner_column = jnp.sum(jnp.where(before == after, owner, 0), axis=1, keepdims=True)
    same = (owner_column == owner) & (before < after)
    rank = jnp.sum(jnp.where(same, 1, 0), axis=0, keepdims=True)
    slots = lax.broadcasted_iota(jnp.int32, (owners * SUBLANES, toks), 0)
    placing[...] = jnp.where(slots == owner * SUBLANES + rank, 1.0, 0.0).astype(jnp.bfloat16)
    pl.semaphore_wait(barrier, owners - 1)
    spread(first, 0)
    weight_copy.wait()
    hidden = convolve(first, 0)
    keep(second, norm_silu(hidden, gains[1:2]))
    spread(second, 1)
    hidden = convolve(second, 1)
    merged = feat[...].reshape(cells, width).astype(jnp.float32) + hidden
    active = norm_silu(merged, gains[2:3]).astype(jnp.bfloat16)
    rest = jnp.zeros((LANES - 4 * width_latent, width), jnp.bfloat16)
    latent_wide = jnp.concatenate([latent_rows[...]] * 4 + [rest], axis=0)
    latent = lax.dot_general(
        active, latent_wide, (((1,), (1,)), ((), ())), preferred_element_type=jnp.float32
    )
    cell = lax.broadcasted_iota(jnp.int32, (cells, LANES), 0)
    lane = lax.broadcasted_iota(jnp.int32, (cells, LANES), 1)
    corner = (cell // cols % 2) * 2 + cell % 2
    alive = (t * frames + cell // (rows * cols) < count[0]) & (corner == 0)
    flagged = jnp.where((lane == 4 * width_latent) & alive, 1.0, 0.0)
    patches = jnp.where(lane // width_latent == corner, latent, flagged).astype(jnp.bfloat16)
    spot = lax.broadcasted_iota(jnp.int32, (toks, cells), 1)
    patch = (spot // (2 * cols)) * (cols // 2) + spot % cols // 2
    mine = patch == lax.broadcasted_iota(jnp.int32, (toks, cells), 0)
    patches = jnp.dot(
        jnp.where(mine, 1.0, 0.0).astype(jnp.bfloat16), patches, preferred_element_type=jnp.float32
    ).astype(jnp.bfloat16)
    outgoing = jnp.dot(
        placing[...], patches, preferred_element_type=jnp.float32
    ).astype(jnp.bfloat16)
    tok_out[...] = outgoing.reshape(owners, SUBLANES, LANES)
    tok_in[pl.ds(me, 1)] = tok_out[pl.ds(me, 1)]

    def tok_copy(source, target):
        return pltpu.make_async_remote_copy(
            src_ref=tok_out.at[target], dst_ref=tok_in.at[source],
            send_sem=tok_send.at[target], recv_sem=tok_recv.at[source],
            device_id={"tm": target // ns, "space": target % ns}, device_id_type=MESH,
        )

    def tok_start(d, carry):
        tok_copy(me, (me + d) % owners).start()
        return carry

    def tok_wait(d, carry):
        o = (me + d) % owners
        tok_copy(o, o).wait_recv()
        return carry

    def tok_sent(d, carry):
        tok_copy(me, (me + d) % owners).wait_send()
        return carry

    lax.fori_loop(1, owners, tok_start, 0)
    spread_sent(first, 0)
    spread_sent(second, 1)
    lax.fori_loop(1, owners, tok_wait, 0)
    row = lax.broadcasted_iota(jnp.int32, (owners * most, owners * SUBLANES), 0)
    held = lax.broadcasted_iota(jnp.int32, (owners * most, owners * SUBLANES), 1)
    inner = held % SUBLANES
    chosen = (row == held // SUBLANES * most + inner) & (inner < most)
    tokens_out[...] = jnp.dot(
        jnp.where(chosen, 1.0, 0.0).astype(jnp.bfloat16),
        tok_in[...].reshape(owners * SUBLANES, LANES),
        preferred_element_type=jnp.float32,
    ).astype(jnp.bfloat16)
    lax.fori_loop(1, owners, tok_sent, 0)


def embedder(channels, tokens, weight, bias, packed):
    held = tokens[...]
    projected = jnp.dot(held[:, :channels], weight[...], preferred_element_type=jnp.float32)
    flags = held[:, channels : channels + 1].astype(jnp.float32)
    packed[...] = ((projected + bias[...]) * flags).astype(jnp.bfloat16)


def shards(
    features,
    frame_counts,
    routes,
    norm_gains,
    conv_weights,
    conv_biases,
    latent_weight,
    embed_weight,
    embed_bias,
):
    feat = features[0]
    frames, rows, cols, width = feat.shape
    cells = frames * rows * cols
    n, ns = lax.axis_size("tm"), lax.axis_size("space")
    owners = n * ns
    out = conv_weights.shape[1]
    pack = max(1, LANES // out)
    latents = latent_weight.shape[1]
    tok_count = routes.shape[1]
    most = (tok_count + owners - 1) // owners + 1
    vmem = pl.BlockSpec(memory_space=pltpu.VMEM)
    dma = pltpu.SemaphoreType.DMA
    field = pltpu.VMEM((n * frames + 2, rows + 2, cols, width), jnp.bfloat16)
    slab = pltpu.VMEM((2, n, cells // pack, pack * out), jnp.bfloat16)
    cuts = CUTS if frames % CUTS == 0 else 1
    tok = pltpu.VMEM((owners, SUBLANES, LANES), jnp.bfloat16)
    tokens = pl.pallas_call(
        functools.partial(encoder, n, ns, most, latents),
        out_shape=jax.ShapeDtypeStruct((owners * most, LANES), jnp.bfloat16),
        in_specs=[vmem, pl.BlockSpec(memory_space=pl.ANY), vmem, vmem, vmem, vmem,
                  pl.BlockSpec(memory_space=pltpu.SMEM)],
        out_specs=vmem,
        scratch_shapes=[
            field, field,
            pltpu.VMEM((2, 9, 3 * out, width), jnp.bfloat16),
            pltpu.VMEM((owners * SUBLANES, tok_count), jnp.bfloat16),
            slab, slab, tok, tok,
            dma,
            dma((2, 2, n, cuts)), dma((2, n, cuts)), dma((2, n, cuts)), dma((2, n, cuts)),
            dma((2, n, cuts)), dma((2, n, cuts)),
            dma((2, n)), dma((2, n)), dma((owners,)), dma((owners,)),
        ],
        compiler_params=pltpu.CompilerParams(collective_id=0, has_side_effects=True),
    )(
        feat,
        conv_weights.transpose(0, 2, 1, 3).reshape(2, 9, 3 * out, width),
        norm_gains,
        conv_biases,
        latent_weight.T,
        routes.reshape(1, tok_count),
        frame_counts,
    )
    channels = 4 * latents
    embed = embed_weight.shape[1]
    chunk = embed // 1 if embed % (1 * LANES) == 0 else embed
    packed = pl.pallas_call(
        functools.partial(embedder, channels),
        grid=(embed // chunk,),
        out_shape=jax.ShapeDtypeStruct((owners * most, embed), jnp.bfloat16),
        in_specs=[
            pl.BlockSpec((owners * most, LANES), lambda i: (0, 0)),
            pl.BlockSpec((channels, chunk), lambda i: (0, i)),
            pl.BlockSpec((1, chunk), lambda i: (0, i)),
        ],
        out_specs=pl.BlockSpec((owners * most, chunk), lambda i: (0, i)),
    )(tokens, embed_weight, embed_bias.reshape(1, embed))
    return packed[None]


def solution(mesh):
    return jax.shard_map(
        shards,
        mesh=mesh,
        in_specs=(
            P(("groups", "clip"), "tm", "space", None, None),
            P(("groups", "clip")),
            P(("groups", "clip"), ("tm", "space"), None),
            P(),
            P(None, "tm", None, None),
            P(),
            P(),
            P(),
            P(),
        ),
        out_specs=P(("groups", "clip"), ("tm", "space"), None),
        check_vma=False,
    )
```
